32 devices in a mesh: row: 4 (over y, x), col: 8 (over z, core).
Axes of the slice: x: 2, y: 2, z: 4, core: 2. Of those that a mesh axis runs over, the one named last changes fastest.
Arguments:
- design: bfloat16 [1024, 24576], P('row', 'col'), may hold values from -6 to 6
- observations: bfloat16 [1024], P('row'), may hold values from -6 to 6
- filter_taps: float32 [64], replicated, may hold values from -0.5 to 0.5
- tap_count: int32 [4], replicated, may hold values from 32 to 64
- arc_id: int32 [1024], replicated, may hold values from 0 to 3, never falling along the last dimension, each value on 1 to 512 neighbouring positions
Outputs:
- normal: float32 [24576, 24576], P('row', 'col')
- right_side: float32 [24576], P('col')
The draws below stay inside these ranges and needn't reach their ends.
Inputs may be any that keep to these rules, and one draw needn't show every extreme that they name: `arc_id`: arc numbers never fall along the epochs; every arc holds 1 to 512 epochs and one holds exactly 512.
All inputs are finite; a program needn't handle non-finite values.
Results may differ from the reference program's by a relative error of at most 0.0031.
Values may be sent and summed in bfloat16 or wider, within the bound.
No kernel may reach another device: no remote copies, remote signals or barrier semaphores. Data moves between devices by JAX's collectives and lax.ppermute only.
A program may use at most 192 MiB of HBM per device.

```python
import math
import jax
import jax.numpy as jnp
import numpy as np
from jax import lax

P_SIZE = 24576
K = 64
ARCS = 4
EPOCHS = 1024
ARC_MOST = 512


def touch_ends(drawn, rng, low, top_value):
    shape = drawn.shape
    spot = [jax.random.randint(jax.random.fold_in(rng, axis), (), 0, shape[axis]) for axis in range(len(shape))]
    drawn = drawn.at[tuple(spot)].set(low)
    longest = shape.index(max(shape))
    spot[longest] = (spot[longest] + 1) % shape[longest]
    return drawn.at[tuple(spot)].set(top_value)


def block_scale(key, extent, split, smallest, high):
    gain = 1.0
    for position, parts in split:
        heights = jax.random.uniform(jax.random.fold_in(jax.random.fold_in(key, 6), position), (parts,), jnp.float32, smallest / len(split), high / len(split))
        gain = gain * jnp.repeat(jnp.exp(heights), extent[position] // parts).reshape((-1,) + (1,) * (len(extent) - 1 - position))
    return gain


def split_up(count, total, most, lean):
    loads = [(1 << 20) // math.isqrt(rank ** lean) + 1 for rank in range(2, count + 1)]
    surplus, given = total - most - (count - 1), [1] * (count - 1)
    while surplus > 0:
        candidates = [i for i in range(count - 1) if given[i] < most]
        whole, remaining = sum([loads[i] for i in candidates]), surplus
        for i in candidates:
            addition = min(most - given[i], max(1, remaining * loads[i] // whole), surplus)
            given[i] = given[i] + addition
            surplus = surplus - addition
    return np.array([most] + given)


def ragged(key, count, total, bound, slope):
    if count == 2:
        one = jax.random.randint(key, (), max(1, total - bound), min(bound, total - 1) + 1)
        return jnp.stack([one, total - one])
    sizes = jnp.asarray(split_up(count, total, bound, slope), jnp.int32)
    pairs = (count - 1) // 2
    giver, receiver = sizes[1:1 + 2 * pairs:2], sizes[2:2 + 2 * pairs:2]
    room = jnp.minimum(giver - 1, bound - receiver)
    moved = jax.random.randint(jax.random.fold_in(key, 1), (pairs,), 0, 1 << 20) % (room + 1)
    sizes = sizes.at[1:1 + 2 * pairs:2].set(giver - moved).at[2:2 + 2 * pairs:2].set(receiver + moved)
    return sizes[jax.random.permutation(jax.random.fold_in(key, 2), count)]


def normal_values(rng, dims, width, bound, cuts=(), held_as=jnp.bfloat16):
    result = jax.random.normal(rng, dims, jnp.float32) * width
    if len(cuts) > 0:
        result = block_scale(rng, dims, cuts, -0.22, 0.18) * result
    return jnp.clip(result, min=-bound, max=bound).astype(held_as)


def setup_inputs(seed: int = 0) -> dict:
    streams_of = jax.random.split(jax.random.key(seed), 6)
    design = normal_values(streams_of[0], (EPOCHS, P_SIZE), 1.0, 6.0, ((0, 4), (1, 8)))
    observations = normal_values(streams_of[1], (EPOCHS,), 1.0, 6.0, ((0, 4),))
    filter_taps = normal_values(streams_of[2], (K,), 0.125, 0.5, (), jnp.float32)
    tap_count = touch_ends(jax.random.randint(streams_of[3], (ARCS,), K // 2, K + 1), jax.random.fold_in(streams_of[3], 1), K // 2, K).astype(jnp.int32)
    arc_id = jnp.searchsorted(jnp.cumsum(ragged(streams_of[4], ARCS, EPOCHS, ARC_MOST, 0)), jnp.arange(EPOCHS), side="right").astype(jnp.int32)
    return dict(design=design, observations=observations, filter_taps=filter_taps, tap_count=tap_count, arc_id=arc_id)


def reference(design, observations, filter_taps, tap_count, arc_id):
    epoch_index = jnp.arange(EPOCHS, dtype=jnp.int32)
    lag_matrix = epoch_index[:, None] - epoch_index[None, :]
    arc_taps = tap_count[arc_id.astype(jnp.int32)].astype(jnp.int32)
    valid_lag = (lag_matrix >= 0) & (lag_matrix < K) & (lag_matrix < arc_taps[:, None])
    valid_lag = valid_lag & (arc_id[:, None] == arc_id[None, :])
    filter_rows = jnp.where(valid_lag, filter_taps[jnp.clip(lag_matrix, 0, K - 1)], jnp.float32(0.0))
    whitened = jnp.dot(filter_rows, design.astype(jnp.float32), precision=lax.Precision.HIGHEST).astype(jnp.bfloat16)
    white_obs = jnp.dot(filter_rows, observations.astype(jnp.float32), precision=lax.Precision.HIGHEST).astype(jnp.bfloat16)
    white_float = whitened.astype(jnp.float32)
    normal = jnp.dot(white_float.T, white_float, precision=lax.Precision.HIGHEST) / EPOCHS
    right_side = jnp.dot(white_obs.astype(jnp.float32), white_float, precision=lax.Precision.HIGHEST) / math.sqrt(EPOCHS)
    return (normal, right_side)
```

```python
import functools
import math

import jax
import jax.numpy as jnp
from jax import lax
from jax.experimental import pallas as pl
from jax.experimental.pallas import tpu as pltpu
from jax.sharding import PartitionSpec as P

LANES = 128
SLICES = 4


def column_slices(cols, count):
    units = cols // LANES
    count = min(count, units)
    cuts = [LANES * (units // count + (i < units % count)) for i in range(count)]
    return [(sum(cuts[:i]), cut) for i, cut in enumerate(cuts)]


def tile_of(extent, most):
    return max(t for t in range(LANES, most + 1, LANES) if extent % t == 0)


def whiten_kernel(slices, taps_ref, arc_t_ref, most_ref, arc_s_ref, halo_ref, design_ref, obs_ref, *refs):
    wide_ref, slice_refs, (ext_ref, obs_ext_ref, split_ref) = refs[0], refs[1:-3], refs[-3:]
    rows, cols = design_ref.shape
    width = halo_ref.shape[0]
    span = ext_ref.shape[0]
    step = LANES
    window = min(span, step + -(-width // LANES) * LANES)
    ext_ref[:width, :] = halo_ref[:, :cols]
    ext_ref[width : width + rows, :] = design_ref[...]
    obs_ext_ref[:width, :] = halo_ref[:, cols:]
    obs_ext_ref[width : width + rows, :] = obs_ref[...]
    if span > width + rows:
        ext_ref[width + rows :, :] = jnp.zeros((span - width - rows, cols), jnp.bfloat16)
        obs_ext_ref[width + rows :, :] = jnp.zeros((span - width - rows, LANES), jnp.bfloat16)
    base = jnp.broadcast_to(taps_ref[...], (rows, span))
    filt = pltpu.roll(base, 0, 1, stride=1, stride_axis=0)
    target = lax.broadcasted_iota(jnp.int32, (rows, span), 0)
    source = lax.broadcasted_iota(jnp.int32, (rows, span), 1)
    lag = target + width - source
    valid = (arc_t_ref[...] == arc_s_ref[...]) & (lag >= 0) & (lag < most_ref[...])
    filt = jnp.where(valid, filt, 0.0)
    high = filt.astype(jnp.bfloat16)
    rest = filt - high.astype(jnp.float32)
    middle = rest.astype(jnp.bfloat16)
    low = (rest - middle.astype(jnp.float32)).astype(jnp.bfloat16)
    split_ref[0] = high
    split_ref[1] = middle
    split_ref[2] = low

    def product(top, data):
        left = [split_ref[i, top : top + step, top : top + window] for i in range(3)]
        small = jnp.dot(left[2], data, preferred_element_type=jnp.float32)
        small = small + jnp.dot(left[1], data, preferred_element_type=jnp.float32)
        return (small + jnp.dot(left[0], data, preferred_element_type=jnp.float32)).astype(jnp.bfloat16)

    for top in range(0, rows, step):
        for slice_ref, (offset, cut) in zip(slice_refs, slices):
            tile = product(top, ext_ref[top : top + window, offset : offset + cut])
            slice_ref[top : top + step, :] = tile
            wide_ref[top : top + step, offset : offset + cut] = tile
        wide_ref[top : top + step, cols:] = product(top, obs_ext_ref[top : top + window, :])


def whiten(slices, taps, arc_t, most, arc_s, halo, design, obs):
    rows, cols = design.shape
    span = arc_s.shape[1]
    vmem = pl.BlockSpec(memory_space=pltpu.VMEM)
    return pl.pallas_call(
        functools.partial(whiten_kernel, slices),
        out_shape=[jax.ShapeDtypeStruct((rows, cols + LANES), jnp.bfloat16)]
        + [jax.ShapeDtypeStruct((rows, cut), jnp.bfloat16) for _, cut in slices],
        in_specs=[vmem] * 7,
        out_specs=[vmem] * (1 + len(slices)),
        scratch_shapes=[
            pltpu.VMEM((span, cols), jnp.bfloat16),
            pltpu.VMEM((span, LANES), jnp.bfloat16),
            pltpu.VMEM((3, rows, span), jnp.bfloat16),
        ],
        name="whiten",
    )(taps, arc_t, most, arc_s, halo, design, obs)


def product_kernel(count, epochs, place_ref, *refs):
    left_refs, right_ref, out_ref = refs[:count], refs[count], refs[-1]
    for i in range(count):

        @pl.when(pl.program_id(0) == i)
        def _():
            out_ref[...] = lax.dot_general(
                left_refs[i][...], right_ref[...], (((0,), (0,)), ((), ())), preferred_element_type=jnp.float32
            ) * (1.0 / epochs)


def product(place, lefts, right, out, shape, offset, cols):
    epochs, cut = lefts[0].shape
    count = len(lefts)
    tile = tile_of(cols, 512)
    rows = tile_of(cut, 1024)
    while offset % rows or cols % rows:
        rows = tile_of(cut, rows - LANES)
    whole = pl.BlockSpec((epochs, rows), lambda i, m, n, place: (0, m))
    in_specs = [whole] * count + [pl.BlockSpec((epochs, tile), lambda i, m, n, place: (0, n))]
    operands = [place, *lefts, right]
    aliases = {}
    if out is not None:
        in_specs.append(pl.BlockSpec(memory_space=pl.ANY))
        operands.append(out)
        aliases = {len(operands) - 1: 0}
    return pl.pallas_call(
        functools.partial(product_kernel, count, epochs),
        out_shape=jax.ShapeDtypeStruct(shape, jnp.float32),
        grid_spec=pltpu.PrefetchScalarGridSpec(
            num_scalar_prefetch=1,
            grid=(count, cut // rows, cols // tile),
            in_specs=in_specs,
            out_specs=pl.BlockSpec(
                (rows, tile), lambda i, m, n, place: (place[i] * (cols // rows) + offset // rows + m, n)
            ),
        ),
        input_output_aliases=aliases,
        cost_estimate=pl.CostEstimate(
            flops=2 * epochs * cut * count * cols,
            bytes_accessed=4 * cut * count * cols + 2 * epochs * cols,
            transcendentals=0,
        ),
        name="product",
    )(*operands)


def on_device(rows_axis, cols_axis, design, observations, filter_taps, tap_count, arc_id):
    layers = cols_axis // rows_axis
    rows_here, cols = design.shape
    width = filter_taps.shape[0]
    epochs = arc_id.shape[0]
    row = lax.axis_index("row")
    col = lax.axis_index("col")
    plane, layer = col // layers, col % layers

    def move(value, target):
        pairs = []
        for r in range(rows_axis):
            for z in range(rows_axis):
                for k in range(layers):
                    place = target(r, z, k)
                    if place is not None:
                        r2, z2, k2 = place
                        pairs.append(((r * rows_axis + z) * layers + k, (r2 * rows_axis + z2) * layers + k2))
        return lax.ppermute(value, ("row", "col"), pairs)

    slices = column_slices(cols, SLICES)
    obs = jnp.pad(observations[:, None], ((0, 0), (0, LANES - 1)))
    tail = jnp.concatenate([design[rows_here - width :], obs[rows_here - width :]], axis=1)
    halo = move(tail, lambda r, z, k: (r + 1, z, k) if r + 1 < rows_axis else None)

    span = -(-(rows_here + width) // LANES) * LANES
    first = row * rows_here
    arc_padded = jnp.concatenate(
        [jnp.full((width,), -1, jnp.int32), arc_id, jnp.full((span - rows_here - width,), -1, jnp.int32)]
    )
    arc_s = lax.dynamic_slice_in_dim(arc_padded, first, span)
    arc_t = lax.dynamic_slice_in_dim(arc_id, first, rows_here)[:, None]
    arc_range = jnp.arange(tap_count.shape[0], dtype=jnp.int32)
    most = jnp.sum(jnp.where(arc_t == arc_range[None, :], tap_count[None, :], 0), axis=1, keepdims=True)
    taps = jnp.pad(filter_taps[::-1], (1, span - width - 1))[None, :]
    wide, *blocks = whiten(slices, taps, arc_t, most, arc_s[None, :], halo, design, obs)

    bits = [1 << b for b in range(rows_axis.bit_length() - 1)]
    own = {0: wide}
    half = (cols + LANES) // (2 * LANES) * LANES
    for i in bits:
        own[i] = move(wide, lambda r, z, k: (r ^ i, z, k))
    for i in range(1, rows_axis):
        if i not in own:
            low, high = i & -i, 1 << (i.bit_length() - 1)
            own[i] = jnp.concatenate(
                [
                    move(own[i ^ low][:, :half], lambda r, z, k: (r ^ low, z, k)),
                    move(own[i ^ high][:, half:], lambda r, z, k: (r ^ high, z, k)),
                ],
                axis=1,
            )
    own_cols = jnp.concatenate([own[i] for i in range(rows_axis)], axis=0)

    shape = (layers * cols, cols)
    place = jnp.stack([layer ^ i for i in range(layers)]).astype(jnp.int32)

    out = None
    for (offset, cut), block in zip(slices, blocks):
        below, above = {}, {}
        for d in range(1, rows_axis):
            hop = d if d <= 2 else 1
            start = d - hop

            def up(r, z, k):
                return (r, z + hop, k) if start <= z and z + hop < rows_axis else None

            def down(r, z, k):
                return (r, z - hop, k) if z < rows_axis - start and z - hop >= 0 else None

            if below[start] is above[start] if start else 2 * hop >= rows_axis:
                held = block if start == 0 else below[start]
                below[d] = above[d] = move(held, lambda r, z, k: up(r, z, k) or down(r, z, k))
            else:
                below[d] = move(block if start == 0 else below[start], up)
                above[d] = move(block if start == 0 else above[start], down)

        def of_plane(p):
            chosen = block
            for d in range(1, rows_axis):
                if below[d] is above[d]:
                    chosen = jnp.where(jnp.abs(plane - p) == d, below[d], chosen)
                else:
                    chosen = jnp.where(plane - p == d, below[d], jnp.where(p - plane == d, above[d], chosen))
            return chosen

        parts = [of_plane(row)]
        for i in range(1, rows_axis):
            parts.append(move(of_plane(row ^ i), lambda r, z, k: (r ^ i, z, k)))
        mine = jnp.concatenate(parts, axis=0)
        lefts = [mine]
        for i in range(1, layers):
            lefts.append(move(mine, lambda r, z, k: (r, z, k ^ i)))
        out = product(place, lefts, own_cols, out, shape, offset, cols)

    right_side = jnp.dot(own_cols[:, cols], own_cols[:, :cols], preferred_element_type=jnp.float32)
    return out, right_side / math.sqrt(epochs)


def solution(mesh):
    return jax.shard_map(
        functools.partial(on_device, mesh.shape["row"], mesh.shape["col"]),
        mesh=mesh,
        in_specs=(P("row", "col"), P("row"), P(), P(), P()),
        out_specs=(P("row", "col"), P("col")),
        check_vma=False,
    )
```

```python
import functools
import math

import jax
import jax.numpy as jnp
from jax import lax
from jax.experimental import pallas as pl
from jax.experimental.pallas import tpu as pltpu
from jax.sharding import PartitionSpec as P

LANES = 128
SLICES = 4
BOTH_LAST = (((1,), (1,)), ((), ()))


def column_slices(cols, count):
    units = cols // LANES
    count = min(count, units)
    cuts = [LANES * (units // count + (i < units % count)) for i in range(count)]
    return [(sum(cuts[:i]), cut) for i, cut in enumerate(cuts)]


def tile_of(most, *extents):
    return max(t for t in range(LANES, most + 1, LANES) if all(extent % t == 0 for extent in extents))


def filters(arc_ref, taps_ref, count_ref, filt_ref):
    chunks, lanes = arc_ref.shape
    window = taps_ref.shape[1]
    history = window - lanes
    arcs = arc_ref[...]
    starts = [
        jnp.sum(jnp.where(arcs < a, 1.0, 0.0), keepdims=True).astype(jnp.int32) for a in range(count_ref.shape[0])
    ]
    base = pltpu.roll(jnp.broadcast_to(taps_ref[...], (window, window)), 0, 1, stride=1, stride_axis=0)[:, :lanes]
    target = lax.broadcasted_iota(jnp.int32, (window, lanes), 1)
    lag = target + history - lax.broadcasted_iota(jnp.int32, (window, lanes), 0)
    epoch = lax.broadcasted_iota(jnp.int32, (1, lanes), 1)
    for j in range(chunks):
        arc = arcs[j : j + 1]
        most = jnp.zeros((1, lanes), jnp.int32)
        for a, start in enumerate(starts):
            most = jnp.where(arc == a, jnp.minimum(count_ref[a], epoch + (j * lanes + 1) - start), most)
        filt = jnp.where((lag >= 0) & (lag < most), base, 0.0).T
        high = filt.astype(jnp.bfloat16)
        rest = filt - high.astype(jnp.float32)
        middle = rest.astype(jnp.bfloat16)
        filt_ref[j, 0] = high
        filt_ref[j, 1] = middle
        filt_ref[j, 2] = (rest - middle.astype(jnp.float32)).astype(jnp.bfloat16)


def three_terms(filt_ref, j, multiply):
    return multiply(filt_ref[j, 2]) + multiply(filt_ref[j, 1]) + multiply(filt_ref[j, 0])


def whiten_kernel(parts, turned, row_ref, count_ref, arc_ref, taps_ref, *refs):
    refs = list(refs)
    obs_ref = None if turned else refs.pop(0)
    piece_refs = [[refs.pop(0) for _ in starts] for starts in parts]
    out_ref = refs.pop(0)
    right_ref = None if turned else refs.pop(0)
    ext_ref, filt_ref = refs[:2]
    chunks, lanes = arc_ref.shape
    window = taps_ref.shape[1]
    history = window - lanes
    rows = piece_refs[0][0].shape[0]
    per_block = rows // lanes
    n = pl.program_id(0)

    @pl.when(n == 0)
    def _():
        filters(arc_ref, taps_ref, count_ref, filt_ref)
        ext_ref[:history, :] = jnp.zeros((history, ext_ref.shape[1]), jnp.bfloat16)
        if not turned:
            white_ref, line_ref = refs[2:]
            for s in range(history // lanes):
                line_ref[s] = jnp.zeros(line_ref.shape[1:], jnp.bfloat16)
            for j in range(chunks):
                here = (j // per_block) ^ row_ref[0]
                line = obs_ref[pl.ds(here * per_block + j % per_block, 1), :]
                line_ref[history // lanes + j] = jnp.broadcast_to(line, line_ref.shape[1:]).astype(jnp.bfloat16)
            for j in range(chunks):
                here = (j // per_block) ^ row_ref[0]
                left = jnp.concatenate([line_ref[j + s] for s in range(window // lanes)], axis=1)
                white = three_terms(
                    filt_ref, j, lambda f: lax.dot_general(left, f, BOTH_LAST, preferred_element_type=jnp.float32)
                )
                at = pl.multiple_of(here * rows + j % per_block * lanes, lanes)
                white_ref[:, pl.ds(at, lanes)] = white.astype(jnp.bfloat16)

    for i, (starts, part_refs) in enumerate(zip(parts, piece_refs)):
        at = pl.multiple_of(history + (row_ref[0] ^ i) * rows, lanes)
        for start, stop, part_ref in zip(starts, [*starts[1:], None], part_refs):
            inside = n >= start if stop is None else (n >= start) & (n < stop)

            @pl.when(inside)
            def _():
                ext_ref[pl.ds(at, rows), :] = part_ref[...]

    for j in range(chunks):
        data = ext_ref[j * lanes : j * lanes + window, :]
        white = three_terms(filt_ref, j, lambda f: jnp.dot(f, data, preferred_element_type=jnp.float32))
        white = white.astype(jnp.bfloat16)
        here = (j // per_block) ^ row_ref[0]
        inner = j % per_block * lanes
        if turned:
            out_ref[here, :, inner : inner + lanes] = white.T
        else:
            out_ref[pl.ds(pl.multiple_of(here * rows + inner, lanes), lanes), :] = white
    if not turned:
        total = jnp.dot(refs[2][...], out_ref[...], preferred_element_type=jnp.float32)
        right_ref[...] = total[:1] * (1.0 / math.sqrt(chunks * lanes))


def whiten(common, pieces, obs=None):
    row_at, count, arcs, taps = common
    turned = obs is None
    chunks, lanes = arcs.shape
    window = taps.shape[1]
    rows = pieces[0][0].shape[0]
    cols = sum(part.shape[1] for part in pieces[0])
    tile = tile_of(256 if turned else 512, *[part.shape[1] for piece in pieces for part in piece])
    epochs = chunks * lanes
    blocks = epochs // rows
    smem = pl.BlockSpec(memory_space=pltpu.SMEM)

    def full(array):
        return pl.BlockSpec(array.shape, lambda n: (0,) * array.ndim)

    in_specs, operands, parts = [smem, smem, full(arcs), full(taps)], [row_at, count, arcs, taps], []
    if not turned:
        in_specs.append(full(obs))
        operands.append(obs)
    for piece in pieces:
        starts = [sum(part.shape[1] for part in piece[:i]) // tile for i in range(len(piece))]
        parts.append(tuple(starts))
        for start, part in zip(starts, piece):
            last = part.shape[1] // tile - 1
            in_specs.append(pl.BlockSpec((rows, tile), lambda n, start=start, last=last: (0, jnp.clip(n - start, 0, last))))
            operands.append(part)
    scratch = [
        pltpu.VMEM((window - lanes + epochs, tile), jnp.bfloat16),
        pltpu.VMEM((chunks, 3, lanes, window), jnp.bfloat16),
    ]
    if turned:
        out_shape = jax.ShapeDtypeStruct((blocks, cols, rows), jnp.bfloat16)
        out_specs = pl.BlockSpec((blocks, tile, rows), lambda n: (0, n, 0))
    else:
        out_shape = [
            jax.ShapeDtypeStruct((epochs, cols), jnp.bfloat16),
            jax.ShapeDtypeStruct((1, cols), jnp.float32),
        ]
        out_specs = [pl.BlockSpec((epochs, tile), lambda n: (0, n)), pl.BlockSpec((1, tile), lambda n: (0, n))]
        scratch += [
            pltpu.VMEM((16, epochs), jnp.bfloat16),
            pltpu.VMEM((chunks + window // lanes - 1, 16, lanes), jnp.bfloat16),
        ]
    return pl.pallas_call(
        functools.partial(whiten_kernel, tuple(parts), turned),
        out_shape=out_shape,
        grid=(cols // tile,),
        in_specs=in_specs,
        out_specs=out_specs,
        scratch_shapes=scratch,
        cost_estimate=pl.CostEstimate(
            flops=6 * epochs * window * cols, bytes_accessed=4 * epochs * cols, transcendentals=0
        ),
        name="whiten_turned" if turned else "whiten",
    )(*operands)


def product_kernel(count, place_ref, *refs):
    left_refs, right_ref, out_ref = refs[:count], refs[count], refs[-1]
    blocks, _, rows = left_refs[0].shape
    for i in range(count):

        @pl.when(pl.program_id(1) == i)
        def _():
            total = None
            for b in range(blocks):
                part = jnp.dot(
                    left_refs[i][b], right_ref[b * rows : (b + 1) * rows, :], preferred_element_type=jnp.float32
                )
                total = part if total is None else total + part
            out_ref[...] = total * (1.0 / (blocks * rows))


def product(place, lefts, right, out, shape, offset):
    blocks, cut, rows = lefts[0].shape
    epochs, cols = right.shape
    count = len(lefts)
    tile = tile_of(512, cols)
    step = tile_of(1024, cut, cols, offset) if offset else tile_of(1024, cut, cols)
    part = pl.BlockSpec((blocks, step, rows), lambda n, i, m, place: (0, m, 0))
    in_specs = [part] * count + [pl.BlockSpec((epochs, tile), lambda n, i, m, place: (0, n))]
    operands = [place, *lefts, right]
    aliases = {}
    if out is not None:
        in_specs.append(pl.BlockSpec(memory_space=pl.ANY))
        operands.append(out)
        aliases = {len(operands) - 1: 0}
    return pl.pallas_call(
        functools.partial(product_kernel, count),
        out_shape=jax.ShapeDtypeStruct(shape, jnp.float32),
        grid_spec=pltpu.PrefetchScalarGridSpec(
            num_scalar_prefetch=1,
            grid=(cols // tile, count, cut // step),
            in_specs=in_specs,
            out_specs=pl.BlockSpec(
                (step, tile), lambda n, i, m, place: (place[i] * (cols // step) + offset // step + m, n)
            ),
        ),
        input_output_aliases=aliases,
        cost_estimate=pl.CostEstimate(
            flops=2 * epochs * cut * count * cols,
            bytes_accessed=4 * cut * count * cols + 2 * epochs * cols,
            transcendentals=0,
        ),
        name="product",
    )(*operands)


def hops(rows_axis):
    shared = {0: False}
    plan = []
    for d in range(1, rows_axis):
        hop = d if d <= 2 else 1
        start = d - hop
        shared[d] = shared[start] if start else 2 * hop >= rows_axis
        plan.append((d, hop, start, shared[d]))
    return plan


def on_device(rows_axis, cols_axis, design, observations, filter_taps, tap_count, arc_id):
    return steps(rows_axis, cols_axis, design, observations, filter_taps, tap_count, arc_id)


def steps(rows_axis, cols_axis, design, observations, filter_taps, tap_count, arc_id):
    layers = cols_axis // rows_axis
    _, cols = design.shape
    width = filter_taps.shape[0]
    row = lax.axis_index("row")
    col = lax.axis_index("col")
    plane, layer = col // layers, col % layers

    def move(value, target):
        pairs = []
        for r in range(rows_axis):
            for z in range(rows_axis):
                for k in range(layers):
                    place = target(r, z, k)
                    if place is not None:
                        r2, z2, k2 = place
                        pairs.append(((r * rows_axis + z) * layers + k, (r2 * rows_axis + z2) * layers + k2))
        return lax.ppermute(value, ("row", "col"), pairs)

    slices = column_slices(cols, SLICES)
    bits = [1 << b for b in range(rows_axis.bit_length() - 1)]

    half = cols // (2 * LANES) * LANES
    own = {0: [design]}
    obs = observations[None, :]
    for i in bits:
        own[i] = [move(design, lambda r, z, k: (r ^ i, z, k))]
        obs = jnp.concatenate([obs, move(obs, lambda r, z, k: (r ^ i, z, k))], axis=0)
    for i in range(1, rows_axis):
        if i not in own:
            low, high = i & -i, 1 << (i.bit_length() - 1)
            first, second = own[i ^ low], own[i ^ high]
            first = first[0] if len(first) > 1 else first[0][:, :half]
            second = second[1] if len(second) > 1 else second[0][:, half:]
            own[i] = [move(first, lambda r, z, k: (r ^ low, z, k)), move(second, lambda r, z, k: (r ^ high, z, k))]

    window = LANES * (1 + -(-width // LANES))
    common = (
        row.reshape(1).astype(jnp.int32),
        tap_count,
        arc_id.reshape(-1, LANES),
        jnp.pad(filter_taps, (LANES, window - LANES - width))[None, :],
    )
    own_cols, right_side = whiten(
        common, [own[i] for i in range(rows_axis)], obs.astype(jnp.float32).reshape(-1, LANES)
    )

    shape = (layers * cols, cols)
    place = jnp.stack([layer ^ i for i in range(layers)]).astype(jnp.int32)

    out = None
    for offset, cut in slices:
        block = design[:, offset : offset + cut]
        below, above = {0: block}, {0: block}
        for d, hop, start, both in hops(rows_axis):

            def up(r, z, k):
                return (r, z + hop, k) if start <= z and z + hop < rows_axis else None

            def down(r, z, k):
                return (r, z - hop, k) if z < rows_axis - start and z - hop >= 0 else None

            if both:
                below[d] = above[d] = move(below[start], lambda r, z, k: up(r, z, k) or down(r, z, k))
            else:
                below[d] = move(below[start], up)
                above[d] = move(above[start], down)

        def of_plane(p):
            chosen = block
            for d in range(1, rows_axis):
                if below[d] is above[d]:
                    chosen = jnp.where(jnp.abs(plane - p) == d, below[d], chosen)
                else:
                    chosen = jnp.where(plane - p == d, below[d], jnp.where(p - plane == d, above[d], chosen))
            return chosen

        pieces = [[of_plane(row)]]
        for i in range(1, rows_axis):
            pieces.append([move(of_plane(row ^ i), lambda r, z, k: (r ^ i, z, k))])
        mine = whiten(common, pieces)
        lefts = [mine] + [move(mine, lambda r, z, k: (r, z, k ^ i)) for i in range(1, layers)]
        out = product(place, lefts, own_cols, out, shape, offset)

    return out, right_side[0]


def solution(mesh):
    rows_axis, cols_axis = mesh.shape["row"], mesh.shape["col"]
    return jax.shard_map(
        functools.partial(on_device, rows_axis, cols_axis),
        mesh=mesh,
        in_specs=(P("row", "col"), P("row"), P(), P(), P()),
        out_specs=(P("row", "col"), P("col")),
        check_vma=False,
    )
```
